32 devices in a mesh: gx: 8 (over z, x), gy: 4 (over y, core).
Axes of the slice: x: 2, y: 2, z: 4, core: 2. Of those that a mesh axis runs over, the one named last changes fastest.
Arguments:
- u_prev: float32 [3, 32, 128, 2048], P(None, None, 'gx', 'gy'), may hold values from -6 to 6
- u_now: float32 [3, 32, 128, 2048], P(None, None, 'gx', 'gy'), may hold values from -6 to 6
- speeds: float32 [2, 32, 128, 2048], P(None, None, 'gx', 'gy'), may hold values from 0.1 to 0.24
- sites: int32 [12288], P(('gx', 'gy')), may hold values from 0 to 8191
- routes: int32 [12288, 1], P(('gx', 'gy')), may hold values from 0 to 31; in each aligned block of 384 rows (0 to 383, 384 to 767, ...) at most 32 rows name the same one
- frame_disp: float32 [240, 32768], P(None, ('gx', 'gy')), may hold values from -4 to 4
- frame_vel: float32 [240, 32768], P(None, ('gx', 'gy')), may hold values from -6 to 6
- frame_acc: float32 [240, 32768], P(None, ('gx', 'gy')), may hold values from -6 to 6
- frame_hyst: float32 [240, 32768], P(None, ('gx', 'gy')), may hold values from -0.5 to 0.5
- frame_kind: int32 [32768], P(('gx', 'gy')), may hold values from 0 to 3
- stiffness: float32 [4, 240, 240], replicated, as said below
Outputs:
- field_before: float32 [3, 32, 128, 2048], P(None, None, 'gx', 'gy')
- field_last: float32 [3, 32, 128, 2048], P(None, None, 'gx', 'gy')
- disp_next: float32 [240, 32768], P(None, ('gx', 'gy'))
- vel_next: float32 [240, 32768], P(None, ('gx', 'gy'))
- acc_next: float32 [240, 32768], P(None, ('gx', 'gy'))
- hyst_next: float32 [240, 32768], P(None, ('gx', 'gy'))
The draws below stay inside these ranges and needn't reach their ends.
Inputs may be any that keep to these rules, and one draw needn't show every extreme that they name: `routes`: among the buildings of one device, no owner is named by more than 32 of them, a bound that some block reaches. `stiffness`: diagonal entries between 1 and 2; off-diagonal entries small.
All inputs are finite; a program needn't handle non-finite values.
Results may differ from the reference program's by a relative error of at most 0.00023.
Values sent between devices are 32-bit elements; how exact they have to be, the bound alone decides.
A program may use at most 192 MiB of HBM per device.

```python
import math
import jax
import jax.numpy as jnp
import numpy as np
from jax import lax

CX = 16
CY = 512
NZ = 32
STEPS = 4
NF = 240
NA = 4
B_DEV = 384
ROWS_DEV = 1024
NX = 128
NY = 2048
BUILDINGS = 12288
SLOTS = 32768
N_GX = 8
N_GY = 4
DEVICES = 32


def draw_stiffness(key, part):
    first_key, second_key = jax.random.split(jax.random.fold_in(key, 11))
    diagonal = jax.random.uniform(first_key, (NA, NF, NF), jnp.float32, 1.0, 2.0)
    off_diag = 0.03 * jax.random.normal(second_key, (NA, NF, NF), jnp.float32)
    identity = jnp.eye(NF, dtype=jnp.float32)[None, :, :]
    return jnp.where(identity > 0.5, diagonal, off_diag).astype(jnp.float32)


def checker_field(key, salt):
    mag_key, noise_key = jax.random.split(jax.random.fold_in(key, salt))
    depth_ids = jnp.arange(NZ, dtype=jnp.int32)[:, None, None]
    east_ids = jnp.arange(NX, dtype=jnp.int32)[None, :, None]
    north_ids = jnp.arange(NY, dtype=jnp.int32)[None, None, :]
    parity = ((depth_ids + east_ids + north_ids) % 2).astype(jnp.float32)
    signs = (1.0 - 2.0 * parity)[None, :, :, :]
    shape = (3, NZ, NX, NY)
    magnitude = jax.random.uniform(mag_key, shape, jnp.float32, 1.5, 4.5)
    noise = jnp.clip(0.6 * jax.random.normal(noise_key, shape, jnp.float32), -1.5, 1.5)
    return (signs * magnitude + noise).astype(jnp.float32)


def draw_u_prev(key, part):
    return checker_field(key, 23)


def draw_u_now(key, part):
    return checker_field(key, 37)


def place_ends(result, rng, least, largest):
    longest = result.shape.index(max(result.shape))
    spots = []
    for shift in (0, 1):
        where = [jax.random.randint(jax.random.fold_in(rng, axis), (), 0, length) for axis, length in enumerate(result.shape)]
        where[longest] = (where[longest] + shift) % result.shape[longest]
        spots.append(tuple(where))
    return result.at[spots[0]].set(least).at[spots[1]].set(largest)


def shard_levels(own_key, shape, cuts, smallest, largest):
    factor_of, own = 1.0, jax.random.fold_in(own_key, 6)
    for position, shards_of in cuts:
        draws = jnp.exp(jax.random.uniform(jax.random.fold_in(own, position), (shards_of,), jnp.float32, smallest / len(cuts), largest / len(cuts)))
        factor_of = factor_of * jnp.repeat(draws, shape[position] // shards_of).reshape([-1 if axis == position else 1 for axis in range(len(shape))])
    return factor_of


def deal_out(own_key, own, number, rows, amount, top, reach, skew):
    sequence = jax.random.permutation(own_key, amount)
    heavy_load, common = shares(amount, rows * top, reach, skew, True), shares(amount, rows * top, reach, skew, False)
    places = jnp.arange(amount)

    def named(tallies, turn):
        used = int((tallies > 0).sum())
        fixed = max(1, used // 4)
        shifted = fixed + (places - fixed + turn * (used - fixed)) % max(1, amount - fixed)
        return jnp.zeros((amount,), jnp.int32).at[sequence[jnp.where(places < fixed, places, shifted)]].set(jnp.asarray(tallies, jnp.int32))

    tallies = jnp.where(number % 4 == 0, named(heavy_load, number // 4), named(common, number - number // 4 - 1))
    mixed = jax.random.permutation(jax.random.fold_in(own, 3), amount)
    donor, sink = mixed[0:amount // 2 * 2:2], mixed[1:amount // 2 * 2:2]
    margin = jnp.minimum(tallies[donor] - 1, reach - tallies[sink]) // 2
    margin = jnp.where((donor == sequence[0]) | (sink == sequence[0]) | (tallies[sink] == 0), 0, jnp.maximum(margin, 0))
    shifted = jax.random.randint(jax.random.fold_in(own, 4), (amount // 2,), 0, 1 << 20) % (margin + 1)
    tallies = tallies.at[donor].add(-shifted).at[sink].add(shifted)
    items = jnp.searchsorted(jnp.cumsum(tallies), jnp.arange(rows * top), side="right").astype(jnp.int32)
    table = items.reshape(top, rows).T
    table = table[jax.random.permutation(jax.random.fold_in(own, 1), rows)]
    turn = jax.random.randint(jax.random.fold_in(own, 2), (rows, 1), 0, top)
    return jnp.take_along_axis(table, (jnp.arange(top)[None, :] + turn) % top, axis=1)


def shares(count, total, most, skew, full):
    loads = [(1 << 20) // math.isqrt(standing ** skew) + 1 for standing in range(1, count + 1)]
    largest = most if full else min(most, max(-(-total // count), total * loads[0] // sum(loads)))
    least = 1 if total - largest >= count - 1 else 0
    counts, spare = [largest] + [least] * (count - 1), total - largest - least * (count - 1)
    while spare > 0:
        movable = [i for i in range(1, count) if counts[i] < largest] or [i for i in range(1, count) if counts[i] < most]
        mass, left = sum([loads[i] for i in movable]), spare
        for i in movable:
            extra = min(most - counts[i], max(1, left * loads[i] // mass), spare)
            counts[i] = counts[i] + extra
            spare = spare - extra
    return np.array(counts)


def gaussian(own_key, extent, scale, reach, pieces=(), held_as=jnp.bfloat16):
    gain = shard_levels(own_key, extent, pieces, -0.22, 0.18) if pieces else 1.0
    values = jax.random.normal(own_key, extent, jnp.float32) * scale * gain
    return jnp.minimum(jnp.maximum(values, -reach), reach).astype(held_as)


def setup_inputs(seed: int = 0) -> dict:
    key_list = jax.random.split(jax.random.key(seed), 12)
    u_prev = draw_u_prev(jax.random.fold_in(key_list[11], 71), 0)
    u_now = draw_u_now(jax.random.fold_in(key_list[11], 71), 0)
    speeds = jnp.clip(jnp.exp(math.log(0.24) - 0.8754687 * jax.random.uniform(key_list[2], (2, NZ, NX, NY), jnp.float32) ** shard_levels(key_list[2], (2, NZ, NX, NY), ((2, 8), (3, 4)), -0.2, 0.2)), 0.1, 0.24)
    sites = place_ends(jax.random.randint(key_list[3], (BUILDINGS,), 0, CX * CY), jax.random.fold_in(key_list[3], 1), 0, (CX * CY) - 1).astype(jnp.int32)
    routes_keys = jax.random.split(jax.random.fold_in(key_list[4], 1), BUILDINGS // B_DEV)
    routes_turns = jax.random.permutation(jax.random.fold_in(key_list[4], 3), BUILDINGS // B_DEV)
    routes = jax.vmap(lambda own, number: deal_out(jax.random.fold_in(key_list[4], 2), own, number, B_DEV, DEVICES, 1, ROWS_DEV // DEVICES, 2))(routes_keys, routes_turns).reshape((BUILDINGS, 1))
    frame_disp = gaussian(key_list[5], (NF, SLOTS), 0.5, 4.0, ((1, 32),), jnp.float32)
    frame_vel = gaussian(key_list[6], (NF, SLOTS), 1.0, 6.0, ((1, 32),), jnp.float32)
    frame_acc = gaussian(key_list[7], (NF, SLOTS), 1.0, 6.0, ((1, 32),), jnp.float32)
    frame_hyst = jnp.clip(jax.random.uniform(key_list[8], (NF, SLOTS), jnp.float32, -0.5, 0.5) * shard_levels(key_list[8], (NF, SLOTS), ((1, 32),), -0.4, 0.0), -0.5, 0.5)
    frame_kind = place_ends(jax.random.randint(key_list[9], (SLOTS,), 0, NA), jax.random.fold_in(key_list[9], 1), 0, NA - 1).astype(jnp.int32)
    stiffness = draw_stiffness(jax.random.fold_in(key_list[11], 71), 0)
    return {"u_prev": u_prev, "u_now": u_now, "speeds": speeds, "sites": sites, "routes": routes, "frame_disp": frame_disp, "frame_vel": frame_vel, "frame_acc": frame_acc, "frame_hyst": frame_hyst, "frame_kind": frame_kind, "stiffness": stiffness}


time_step = 0.5
damping = 0.1
yield_drift = 0.5
hyst_stiff = 1.0
ground_gain = 0.1


def trim_rim(array, dims, width):
    for dim in dims:
        array = lax.slice_in_dim(array, width, array.shape[dim] - width, axis=dim)
    return array


def second_diff(padded, dim):
    length = padded.shape[dim]

    def part(start):
        return lax.slice_in_dim(padded, start, length - 4 + start, axis=dim)

    return (16.0 * (part(1) + part(3)) - (part(0) + part(4)) - 30.0 * part(2)) / 12.0


def wave_accel(padded, speeds):
    along_depth = trim_rim(second_diff(padded, 1), (2, 3), 2)
    along_east = trim_rim(second_diff(padded, 2), (1, 3), 2)
    along_north = trim_rim(second_diff(padded, 3), (1, 2), 2)
    own_term = jnp.stack([along_east[0], along_north[1], along_depth[2]])
    total = along_east + along_north + along_depth
    return speeds[0] * own_term + speeds[1] * (total - own_term)


def shift_down(values):
    return jnp.concatenate([jnp.zeros_like(values[:3]), values[:-3]], axis=0)


def shift_up(values):
    return jnp.concatenate([values[3:], jnp.zeros_like(values[:3])], axis=0)


def frame_step(slot_motion, frame_disp, frame_vel, frame_acc, frame_hyst, frame_kind, stiffness):
    disp_next = frame_disp + time_step * frame_vel + 0.5 * time_step * time_step * frame_acc
    drift_change = (disp_next - shift_down(disp_next)) - (frame_disp - shift_down(frame_disp))
    hyst_next = jnp.clip(frame_hyst + drift_change, -yield_drift, yield_drift)
    elastic = jnp.zeros_like(disp_next)
    for kind in range(stiffness.shape[0]):
        product = jnp.dot(stiffness[kind], disp_next, precision=lax.Precision.HIGHEST)
        elastic = elastic + jnp.where(frame_kind[None, :] == kind, product, 0.0)
    forcing = jnp.tile(slot_motion, (frame_disp.shape[0] // 3, 1))
    acc_next = (-forcing - damping * (frame_vel + 0.5 * time_step * frame_acc) - elastic
                - hyst_stiff * (hyst_next - shift_up(hyst_next)))
    vel_next = frame_vel + 0.5 * time_step * (frame_acc + acc_next)
    return disp_next, vel_next, acc_next, hyst_next


def reference(u_prev, u_now, speeds, sites, routes, frame_disp, frame_vel, frame_acc, frame_hyst, frame_kind, stiffness):
    levels = [u_prev, u_now]
    for step in range(STEPS):
        padded = jnp.pad(levels[-1], ((0, 0), (2, 2), (2, 2), (2, 2)))
        levels.append(2.0 * levels[-1] - levels[-2] + wave_accel(padded, speeds))
    ground = ground_gain * (levels[-1] - 2.0 * levels[-2] + levels[-3])[:, 0]
    devices = N_GX * N_GY
    holder = jnp.arange(devices * B_DEV, dtype=jnp.int32) // B_DEV
    row_cell = (holder // N_GY) * CX + sites // CY
    col_cell = (holder % N_GY) * CY + sites % CY
    motion = ground[:, row_cell, col_cell]
    target_dev = routes[:, 0].reshape(devices, B_DEV)
    onehot = (target_dev[:, :, None] == jnp.arange(devices, dtype=jnp.int32)[None, None, :]).astype(jnp.int32)
    before = jnp.cumsum(onehot, axis=1) - onehot
    rank = jnp.sum(before * onehot, axis=2)
    source = jnp.arange(devices, dtype=jnp.int32)[:, None]
    capacity = ROWS_DEV // devices
    target = (target_dev * ROWS_DEV + source * capacity + rank).reshape(-1).astype(jnp.int32)
    slot_motion = jnp.zeros((3, devices * ROWS_DEV), jnp.float32).at[:, target].set(motion)
    disp_next, vel_next, acc_next, hyst_next = frame_step(slot_motion, frame_disp, frame_vel, frame_acc, frame_hyst, frame_kind, stiffness)
    return levels[-2], levels[-1], disp_next, vel_next, acc_next, hyst_next
```

```python
import functools

import jax
import jax.numpy as jnp
from jax import lax
from jax.experimental import pallas as pl
from jax.experimental.pallas import tpu as pltpu
from jax.sharding import PartitionSpec as P

STEPS = 4
time_step = 0.5
damping = 0.1
yield_drift = 0.5
hyst_stiff = 1.0
ground_gain = 0.1
LANES = 128
TOP = 8
GROUP = 2
SPAN = 4
HIGHEST = lax.Precision.HIGHEST
MESH = pl.DeviceIdType.MESH


def lines(n_gx, n_gy):
    return (("gy", n_gy), ("gx", n_gx))


def split(values):
    high = values.astype(jnp.bfloat16)
    return high, (values - high.astype(jnp.float32)).astype(jnp.bfloat16)


def product(a, b):
    return jnp.dot(a, b, preferred_element_type=jnp.float32)


def wave_kernel(
    n_gx, n_gy, capacity,
    u_prev, u_now, speeds, sites, routes,
    frame_disp, frame_vel, frame_acc, frame_hyst, frame_kind, stiffness,
    lev_a, lev_b, fd, f_vel, f_acc, fh,
    spd, stiff, stiff_high, stiff_low, site_row, route_row, kind_row,
    pick, placing, ground, send_1, recv_1, send_2, recv_2, moved,
    load_sem, xs_sem, xr_sem, ys_sem, yr_sem,
    send_1_sem, recv_1_sem, send_2_sem, recv_2_sem,
):
    ncomp, nz, cx, cy = u_now.shape
    tiles = cy // LANES
    place = {"gx": lax.axis_index("gx"), "gy": lax.axis_index("gy")}
    gx, gy = place["gx"], place["gy"]
    has = (gx > 0, gx < n_gx - 1, gy > 0, gy < n_gy - 1)
    peer = ({"gx": gx - 1}, {"gx": gx + 1}, {"gy": gy - 1}, {"gy": gy + 1})

    loads = []

    def load(src, dst):
        copy = pltpu.make_async_copy(src, dst, load_sem.at[len(loads)])
        copy.start()
        loads.append(copy)
        return copy

    inner = pl.ds(TOP, cx)

    def load_field(src, c, lev):
        return [
            load(
                src.at[c, :, :, pl.ds(t * LANES, LANES)],
                lev.at[c, pl.ds(2, nz), t + 1, inner],
            )
            for t in range(tiles)
        ]

    now_in = [load_field(u_now, c, lev_b) for c in range(ncomp)]
    speeds_in = [
        load(speeds.at[s, :, :, pl.ds(t * LANES, LANES)], spd.at[s, :, t])
        for s in range(2)
        for t in range(tiles)
    ]
    prev_in = [load_field(u_prev, c, lev_a) for c in range(ncomp)]
    frames_in = [
        load(frame_disp, fd), load(frame_vel, f_vel), load(frame_acc, f_acc),
        load(frame_hyst, fh), load(stiffness, stiff), load(frame_kind, kind_row),
    ]
    places_in = [load(sites, site_row), load(routes, route_row)]

    barrier = pltpu.get_barrier_semaphore()
    for axis, size in lines(n_gx, n_gy):
        for off in range(1, size):
            pl.semaphore_signal(
                barrier, inc=1, device_id={axis: lax.rem(place[axis] + off, size)},
                device_id_type=MESH,
            )

    rim = jnp.zeros((tiles, cx, LANES), jnp.float32)
    for lev in (lev_a, lev_b):
        for c in range(ncomp):
            for z in (0, 1, nz + 2, nz + 3):
                lev[c, z, pl.ds(1, tiles), inner] = rim

    def clear(body):
        def step(z, carry):
            for lev in (lev_a, lev_b):
                for c in range(ncomp):
                    body(lev, c, z + 2)
            return carry

        lax.fori_loop(0, nz, step, 0)

    for side in range(2):
        @pl.when(jnp.logical_not(has[side]))
        def _(side=side):
            rows = pl.ds((TOP - 2, TOP + cx)[side], 2)
            def body(lev, c, z):
                lev[c, z, pl.ds(1, tiles), rows] = jnp.zeros((tiles, 2, LANES), jnp.float32)
            clear(body)

        @pl.when(jnp.logical_not(has[2 + side]))
        def _(side=side):
            at = (0, tiles + 1)[side]
            def body(lev, c, z):
                lev[c, z, at, inner] = jnp.zeros((cx, LANES), jnp.float32)
            clear(body)

    pl.semaphore_wait(barrier, n_gx + n_gy - 2)

    def planes(k, t):
        cut = 2 * (STEPS - k) - 1
        return (0, cut) if t == 0 else (cut, nz)

    def levels(k):
        return (lev_a, lev_b) if k % 2 == 0 else (lev_b, lev_a)

    def halo_copy(k, c, t, d, sending):
        lev = levels(k)[1]
        low, high = planes(k, t)
        zs = pl.ds(low + 2, high - low)
        if d < 2:
            from_row, to_row = ((TOP, TOP + cx), (TOP + cx - 2, TOP - 2))[d]
            src = lev.at[c, zs, pl.ds(1, tiles), pl.ds(from_row, 2)]
            dst = lev.at[c, zs, pl.ds(1, tiles), pl.ds(to_row, 2)]
            ss, rs = xs_sem, xr_sem
        else:
            from_tile, to_tile = ((1, tiles + 1), (tiles, 0))[d - 2]
            src = lev.at[c, zs, from_tile, inner]
            dst = lev.at[c, zs, to_tile, inner]
            ss, rs = ys_sem, yr_sem
        mine = d % 2
        return pltpu.make_async_remote_copy(
            src_ref=src, dst_ref=dst,
            send_sem=ss.at[k, c, t, mine], recv_sem=rs.at[k, c, t, 1 - mine],
            device_id=peer[d if sending else d ^ 1], device_id_type=MESH,
        )

    def send_halo(k, c, t):
        for d in range(4):
            @pl.when(has[d])
            def _(d=d):
                halo_copy(k, c, t, d, True).start()

    def wait_halo(k, c, t):
        for d in range(4):
            @pl.when(has[d ^ 1])
            def _(d=d):
                halo_copy(k, c, t, d, False).wait_recv()

    def wait_sent(k, c, t):
        for d in range(4):
            @pl.when(has[d])
            def _(d=d):
                halo_copy(k, c, t, d, True).wait_send()

    lane = lax.broadcasted_iota(jnp.int32, (SPAN, cx, LANES), 2)

    def each_plane(low, high, body):
        whole = (high - low) // GROUP

        def group(i, carry):
            for j in range(GROUP):
                body(low + i * GROUP + j)
            return carry

        if whole:
            lax.fori_loop(0, whole, group, 0)
        for z in range(low + whole * GROUP, high):
            body(z)

    def wave_part(k, c, low, high):
        older, newer = levels(k)

        def plane(z):
            for first in range(0, tiles, SPAN):
                mid = pl.ds(first + 1, SPAN)
                u = newer[c, z + 2, mid, inner]
                before = newer[c, z + 2, pl.ds(first, SPAN), inner]
                after = newer[c, z + 2, pl.ds(first + 2, SPAN), inner]

                deep_1 = newer[c, z + 1, mid, inner] + newer[c, z + 3, mid, inner]
                deep_2 = newer[c, z, mid, inner] + newer[c, z + 4, mid, inner]
                east_1 = (
                    newer[c, z + 2, mid, pl.ds(TOP - 1, cx)] + newer[c, z + 2, mid, pl.ds(TOP + 1, cx)]
                )
                east_2 = (
                    newer[c, z + 2, mid, pl.ds(TOP - 2, cx)] + newer[c, z + 2, mid, pl.ds(TOP + 2, cx)]
                )
                north_1 = (
                    pltpu.roll(jnp.where(lane == LANES - 1, before, u), 1, 2)
                    + pltpu.roll(jnp.where(lane == 0, after, u), LANES - 1, 2)
                )
                north_2 = (
                    pltpu.roll(jnp.where(lane >= LANES - 2, before, u), 2, 2)
                    + pltpu.roll(jnp.where(lane < 2, after, u), LANES - 2, 2)
                )
                ones, twos = [east_1, north_1, deep_1], [east_2, north_2, deep_2]
                own = 16.0 * ones.pop(c) - twos.pop(c)
                other = 16.0 * (ones[0] + ones[1]) - (twos[0] + twos[1])
                at = pl.ds(first, SPAN)
                old = older[c, z + 2, mid, inner]
                v = (spd[2, z, at] * u - old) + (spd[0, z, at] * own + spd[1, z, at] * other)
                older[c, z + 2, mid, inner] = v
                if k == STEPS - 1 and isinstance(z, int) and z == 0:
                    g = ground_gain * (v - 2.0 * u + old)
                    for i in range(SPAN):
                        ground[pl.ds(c * cx, cx), pl.ds((first + i) * LANES, LANES)] = g[i]

        each_plane(low, high, plane)

    def scale_speeds(z, carry):
        own, other = spd[0, z] * (1.0 / 12.0), spd[1, z] * (1.0 / 12.0)
        spd[0, z] = own
        spd[1, z] = other
        spd[2, z] = 2.0 - 30.0 * own - 60.0 * other
        return carry

    def top_step(k, c):
        wait_halo(k, c, 0)
        if k > 0:
            wait_sent(k - 1, c, 0)
        low, high = planes(k, 0)
        wave_part(k, c, low, high)
        if k < STEPS - 1:
            send_halo(k + 1, c, 0)

    def deep_step(k, c):
        wait_halo(k, c, 1)
        if k > 0:
            wait_sent(k - 1, c, 1)
        low, high = planes(k, 1)
        wave_part(k, c, low, high)
        if k < STEPS - 1:
            send_halo(k + 1, c, 1)

    nf, slots = fd.shape
    wide = 2 * LANES

    def frames(i, carry):
        cols = pl.ds(pl.multiple_of(i * wide, wide), wide)
        frow = lax.broadcasted_iota(jnp.int32, (nf, wide), 0)
        d0, v0, a0 = fd[:, cols], f_vel[:, cols], f_acc[:, cols]
        change = time_step * v0 + 0.5 * time_step * time_step * a0
        nxt = d0 + change
        moving = nxt - d0
        drift = moving - jnp.where(frow < 3, 0.0, pltpu.roll(moving, 3, 0))
        hyst = jnp.clip(fh[:, cols] + drift, -yield_drift, yield_drift)
        fd[:, cols] = nxt
        fh[:, cols] = hyst
        kinds = kind_row[:, cols]
        total = (-damping) * (v0 + 0.5 * time_step * a0) - hyst_stiff * (
            hyst - jnp.where(frow >= nf - 3, 0.0, pltpu.roll(hyst, nf - 3, 0))
        )
        high, low = split(nxt)
        for kind in range(stiff.shape[0]):
            found = product(stiff_high[kind], high) + (
                product(stiff_high[kind], low) + product(stiff_low[kind], high)
            )
            total = total - jnp.where(kinds == kind, found, 0.0)
        f_acc[:, cols] = total
        f_vel[:, cols] = v0 + 0.5 * time_step * (a0 + total)
        return carry

    def split_stiffness():
        for kind in range(stiff.shape[0]):
            high, low = split(stiff[kind])
            stiff_high[kind] = high
            stiff_low[kind] = low

    def locate():
        count = route_row.shape[1]
        route = route_row[...]
        pick[...] = (
            lax.broadcasted_iota(jnp.int32, (cy, count), 0) == (site_row[...] & (cy - 1))
        ).astype(jnp.float32)
        named = (
            lax.broadcasted_iota(jnp.int32, (n_gx * n_gy, count), 0) == route
        ).astype(jnp.float32)
        earlier = (
            lax.broadcasted_iota(jnp.int32, (count, count), 0)
            < lax.broadcasted_iota(jnp.int32, (count, count), 1)
        ).astype(jnp.float32)
        ahead = jnp.dot(named, earlier, precision=HIGHEST, preferred_element_type=jnp.float32)
        rank = jnp.sum(ahead * named, axis=0, keepdims=True).astype(jnp.int32)
        owner_x = route >> (n_gy.bit_length() - 1)
        owner_y = route & (n_gy - 1)
        spot = owner_y * (n_gx * capacity) + owner_x * capacity + rank
        placing[...] = (
            lax.broadcasted_iota(jnp.int32, (slots, count), 0) == spot
        ).astype(jnp.float32)

    def parcel(axis, size, send, recv, ss, rs, off, sending):
        me = place[axis]
        to = lax.rem(me + off, size)
        source = lax.rem(me + size - off, size)
        return pltpu.make_async_remote_copy(
            src_ref=send.at[to],
            dst_ref=recv.at[me if sending else source],
            send_sem=ss.at[off], recv_sem=rs.at[off],
            device_id={axis: to}, device_id_type=MESH,
        )

    hop_1 = ("gy", n_gy, send_1, recv_1, send_1_sem, recv_1_sem)
    hop_2 = ("gx", n_gx, send_2, recv_2, send_2_sem, recv_2_sem)

    def start_hop(hop):
        axis, size, send, recv = hop[:4]
        for off in range(1, size):
            parcel(*hop, off, True).start()
        recv[place[axis]] = send[place[axis]]

    def end_hop(hop):
        for off in range(1, hop[1]):
            parcel(*hop, off, False).wait_recv()

    def post_motion():
        count = route_row.shape[1]
        cells = jnp.dot(
            ground[...], pick[...], precision=HIGHEST, preferred_element_type=jnp.float32
        )
        at_row = lax.broadcasted_iota(jnp.int32, (cx, count), 0) == (
            site_row[...] >> (cy.bit_length() - 1)
        )
        motion = jnp.concatenate(
            [
                jnp.sum(jnp.where(at_row, cells[c * cx:(c + 1) * cx], 0.0), axis=0, keepdims=True)
                for c in range(ncomp)
            ]
            + [jnp.zeros((8 - ncomp, count), jnp.float32)],
            axis=0,
        )
        outgoing = lax.dot_general(
            motion, placing[...], (((1,), (1,)), ((), ())),
            precision=HIGHEST, preferred_element_type=jnp.float32,
        )
        width = n_gx * capacity
        for y in range(n_gy):
            send_1[y] = outgoing[:, y * width:(y + 1) * width]
        start_hop(hop_1)

    part = n_gy * capacity
    narrow = lax.broadcasted_iota(jnp.int32, (8, LANES), 1)

    def relay_motion():
        end_hop(hop_1)
        for x in range(n_gx):
            tile, start = divmod(x * capacity, LANES)
            total = jnp.zeros((8, LANES), jnp.float32)
            for y in range(n_gy):
                piece = recv_1[y, :, tile * LANES:(tile + 1) * LANES]
                shift = (y * capacity - start) % LANES
                if shift:
                    piece = pltpu.roll(piece, shift, 1)
                here = jnp.logical_and(narrow >= y * capacity, narrow < (y + 1) * capacity)
                total = jnp.where(here, piece, total)
            send_2[x] = total
        start_hop(hop_2)

    def add_forcing():
        end_hop(hop_2)
        per_tile = LANES // part
        for tile in range(slots // LANES):
            total = recv_2[tile * per_tile]
            for i in range(1, per_tile):
                piece = pltpu.roll(recv_2[tile * per_tile + i], i * part, 1)
                total = jnp.where(narrow >= i * part, piece, total)
            moved[:, tile * LANES:(tile + 1) * LANES] = total

        def chunk(i, carry):
            cols = pl.ds(pl.multiple_of(i * LANES, LANES), LANES)
            ids = lax.broadcasted_iota(jnp.int32, (nf, LANES), 0)
            phase = ids - 3 * ((ids * 43691) >> 17)
            m = moved[:, cols]
            force = jnp.where(phase == 0, m[0:1], jnp.where(phase == 1, m[1:2], m[2:3]))
            f_acc[:, cols] = f_acc[:, cols] - force
            f_vel[:, cols] = f_vel[:, cols] - (0.5 * time_step) * force
            return carry

        lax.fori_loop(0, slots // LANES, chunk, 0)

    for c in range(ncomp):
        for copy in now_in[c]:
            copy.wait()
        send_halo(0, c, 0)
    send_halo(0, 0, 1)
    for copy in speeds_in:
        copy.wait()
    lax.fori_loop(0, nz, scale_speeds, 0)
    for c in range(ncomp):
        for copy in prev_in[c]:
            copy.wait()
        top_step(0, c)
    send_halo(0, 1, 1)
    for copy in places_in:
        copy.wait()
    locate()
    for c in range(ncomp):
        top_step(1, c)
    send_halo(0, 2, 1)
    deep_step(0, 0)
    for c in range(ncomp):
        top_step(2, c)
    deep_step(0, 1)
    for c in range(ncomp):
        top_step(3, c)
    post_motion()
    deep_step(0, 2)
    for copy in frames_in:
        copy.wait()
    split_stiffness()
    lax.fori_loop(0, slots // wide, frames, 0)
    deep_step(1, 0)
    relay_motion()
    deep_step(1, 1)
    deep_step(1, 2)
    deep_step(2, 0)
    add_forcing()
    deep_step(2, 1)
    deep_step(2, 2)
    for c in range(ncomp):
        deep_step(3, c)
    for c in range(ncomp):
        for t in range(2):
            wait_sent(STEPS - 1, c, t)
    for hop in (hop_1, hop_2):
        for off in range(1, hop[1]):
            parcel(*hop, off, True).wait_send()


def finish_kernel(lev_a, lev_b, fd, f_vel, f_acc, fh, before, last, disp, vel, acc, hyst, sem):
    ncomp, nz, cx, cy = before.shape
    copies = []

    def store(src, dst):
        copy = pltpu.make_async_copy(src, dst, sem.at[len(copies)])
        copy.start()
        copies.append(copy)

    for lev, out in ((lev_a, before), (lev_b, last)):
        for c in range(ncomp):
            for t in range(cy // LANES):
                store(
                    lev.at[c, pl.ds(2, nz), t + 1, pl.ds(TOP, cx)],
                    out.at[c, :, :, pl.ds(t * LANES, LANES)],
                )
    for src, dst in ((fd, disp), (f_vel, vel), (f_acc, acc), (fh, hyst)):
        store(src, dst)
    for copy in copies:
        copy.wait()


def shards(
    n_gx, n_gy,
    u_prev, u_now, speeds, sites, routes,
    frame_disp, frame_vel, frame_acc, frame_hyst, frame_kind, stiffness,
):
    ncomp, nz, cx, cy = u_now.shape
    devices = n_gx * n_gy
    nf, slots = frame_disp.shape
    capacity = slots // devices
    count = sites.shape[0]
    tiles = cy // LANES
    f32 = jnp.float32
    i32 = jnp.int32
    bf16 = jnp.bfloat16
    level = pltpu.VMEM((ncomp, nz + 4, tiles + 2, cx + 2 * TOP, LANES), f32)
    batch = pltpu.VMEM((nf, slots), f32)
    first_hop = pltpu.VMEM((n_gy, 8, n_gx * capacity), f32)
    second_hop = pltpu.VMEM((n_gx, 8, LANES), f32)
    halo_sem = pltpu.SemaphoreType.DMA((STEPS, ncomp, 2, 2))
    hbm = pl.BlockSpec(memory_space=pltpu.HBM)
    vmem = pl.BlockSpec(memory_space=pltpu.VMEM)
    held = pl.pallas_call(
        functools.partial(wave_kernel, n_gx, n_gy, capacity),
        out_shape=(level, level, batch, batch, batch, batch),
        in_specs=[hbm] * 11,
        out_specs=(vmem,) * 6,
        scratch_shapes=[
            pltpu.VMEM((3, nz, tiles, cx, LANES), f32),
            pltpu.VMEM(stiffness.shape, f32),
            pltpu.VMEM(stiffness.shape, bf16), pltpu.VMEM(stiffness.shape, bf16),
            pltpu.VMEM((1, count), i32), pltpu.VMEM((1, count), i32), pltpu.VMEM((1, slots), i32),
            pltpu.VMEM((cy, count), f32), pltpu.VMEM((slots, count), f32),
            pltpu.VMEM((ncomp * cx, cy), f32), first_hop, first_hop, second_hop, second_hop,
            pltpu.VMEM((8, slots), f32),
            pltpu.SemaphoreType.DMA((2 * ncomp * tiles + 2 * tiles + 8,)),
            halo_sem, halo_sem, halo_sem, halo_sem,
            pltpu.SemaphoreType.DMA((n_gy,)), pltpu.SemaphoreType.DMA((n_gy,)),
            pltpu.SemaphoreType.DMA((n_gx,)), pltpu.SemaphoreType.DMA((n_gx,)),
        ],
        compiler_params=pltpu.CompilerParams(
            collective_id=0, has_side_effects=True, vmem_limit_bytes=32 * 1024 * 1024
        ),
        name="wave",
    )(
        u_prev, u_now, speeds, sites.reshape(1, count), routes.reshape(1, count),
        frame_disp, frame_vel, frame_acc, frame_hyst, frame_kind.reshape(1, slots), stiffness,
    )
    field = jax.ShapeDtypeStruct(u_now.shape, f32)
    frame = jax.ShapeDtypeStruct(frame_disp.shape, f32)
    return pl.pallas_call(
        finish_kernel,
        out_shape=(field, field, frame, frame, frame, frame),
        in_specs=[vmem] * 6,
        out_specs=(hbm,) * 6,
        scratch_shapes=[pltpu.SemaphoreType.DMA((2 * ncomp * tiles + 4,))],
        compiler_params=pltpu.CompilerParams(
            has_side_effects=True, vmem_limit_bytes=1024 * 1024
        ),
        name="finish",
    )(*held)


def solution(mesh):
    cells = P(None, None, "gx", "gy")
    both = ("gx", "gy")
    frame = P(None, both)
    return jax.shard_map(
        functools.partial(shards, mesh.shape["gx"], mesh.shape["gy"]),
        mesh=mesh,
        in_specs=(cells, cells, cells, P(both), P(both, None), frame, frame, frame, frame,
                  P(both), P()),
        out_specs=(cells, cells, frame, frame, frame, frame),
        check_vma=False,
    )
```

```python
import functools

import jax
import jax.numpy as jnp
from jax import lax
from jax.experimental import pallas as pl
from jax.experimental.pallas import tpu as pltpu
from jax.sharding import PartitionSpec as P

STEPS = 4
time_step = 0.5
damping = 0.1
yield_drift = 0.5
hyst_stiff = 1.0
ground_gain = 0.1
LANES = 128
SUB = 8
TOP = 8
GROUP = 8
TAIL = 2
HIGHEST = lax.Precision.HIGHEST
MESH = pl.DeviceIdType.MESH


def lines(n_gx, n_gy):
    return (("gy", n_gy), ("gx", n_gx))


def split(values):
    high = values.astype(jnp.bfloat16)
    return high, (values - high.astype(jnp.float32)).astype(jnp.bfloat16)


def product(a, b):
    return jnp.dot(a, b, preferred_element_type=jnp.float32)


def each_group(low, high, body):
    whole = (high - low) // GROUP
    rest = low + whole * GROUP

    def group(i, carry):
        body(low + i * GROUP, GROUP)
        return carry

    if whole > 1:
        lax.fori_loop(0, whole, group, 0)
    elif whole:
        body(low, GROUP)
    if rest < high:
        body(rest, high - rest)


def next_level(newer, older, spd, c, start, count, put):
    tiles, cx = newer.shape[2] - 2, newer.shape[3] - 2 * TOP
    lane = lax.broadcasted_iota(jnp.int32, (SUB, LANES), 1)
    for half in range(cx // SUB):
        at = TOP + half * SUB
        rows, local = pl.ds(at, SUB), pl.ds(half * SUB, SUB)
        seen = {}

        def get(t, p):
            if (t, p) not in seen:
                seen[t, p] = newer[c, start + p + 2, t, rows]
            return seen[t, p]

        for t in range(1, tiles + 1):
            for p in range(count):
                u = get(t, p)

                def moved(shift):
                    return newer[c, start + p + 2, t, pl.ds(at + shift, SUB)]

                def turned(i):
                    low = jnp.where(lane >= LANES - i, get(t - 1, p), u)
                    high = jnp.where(lane < i, get(t + 1, p), u)
                    return pltpu.roll(low, i, 1) + pltpu.roll(high, LANES - i, 1)

                ones, twos = [
                    [moved(-i) + moved(i), turned(i), get(t, p - i) + get(t, p + i)]
                    for i in (1, 2)
                ]
                own = 16.0 * ones.pop(c) - twos.pop(c)
                other = 16.0 * (ones[0] + ones[1]) - (twos[0] + twos[1])
                keep, along, across = [spd[i, start + p, t - 1, local] for i in (2, 0, 1)]
                old = older[c, start + p + 2, t, rows]
                v = (keep * u - old) + (along * own + across * other)
                put(p, t, half, v, u, old)


def wave_kernel(
    n_gx, n_gy, capacity,
    u_prev, u_now, speeds, sites, routes,
    frame_disp, frame_vel, frame_acc, frame_hyst, frame_kind, stiffness,
    lev_a, lev_b, spd, fd, f_vel, f_acc, fh,
    stiff, stiff_high, stiff_low, site_list, route_row, kind_list,
    pick, placing, ground, send_1, recv_1, send_2, recv_2, moved,
    load_sem, xs_sem, xr_sem, ys_sem, yr_sem, pass_sem, forward_sem,
    send_1_sem, recv_1_sem, send_2_sem, recv_2_sem,
):
    ncomp, nz, cx, cy = u_now.shape
    tiles = cy // LANES
    nf, slots = fd.shape
    place = {"gx": lax.axis_index("gx"), "gy": lax.axis_index("gy")}
    gx, gy = place["gx"], place["gy"]
    has = (gx > 0, gx < n_gx - 1, gy > 0, gy < n_gy - 1)
    peer = ({"gx": gx - 1}, {"gx": gx + 1}, {"gy": gy - 1}, {"gy": gy + 1})

    loads = []

    def load(src, dst):
        copy = pltpu.make_async_copy(src, dst, load_sem.at[len(loads)])
        copy.start()
        loads.append(copy)
        return copy

    inner = pl.ds(TOP, cx)

    def load_field(src, c, lev):
        return [
            load(
                src.at[c, :, :, pl.ds(t * LANES, LANES)],
                lev.at[c, pl.ds(2, nz), t + 1, inner],
            )
            for t in range(tiles)
        ]

    places_in = [load(sites, site_list), load(routes, route_row)]
    now_in = [load_field(u_now, c, lev_b) for c in range(ncomp)]
    speeds_in = [
        load(speeds.at[s, :, :, pl.ds(t * LANES, LANES)], spd.at[s, :, t])
        for s in range(2)
        for t in range(tiles)
    ]
    prev_in = [load_field(u_prev, c, lev_a) for c in range(ncomp)]
    frames_in = [
        load(frame_disp, fd), load(frame_vel, f_vel), load(frame_acc, f_acc),
        load(frame_hyst, fh), load(stiffness, stiff), load(frame_kind, kind_list),
    ]

    barrier = pltpu.get_barrier_semaphore()
    for axis, size in lines(n_gx, n_gy):
        for off in range(1, size):
            pl.semaphore_signal(
                barrier, inc=1, device_id={axis: lax.rem(place[axis] + off, size)},
                device_id_type=MESH,
            )

    rim = jnp.zeros((tiles, cx, LANES), jnp.float32)
    for lev in (lev_a, lev_b):
        for c in range(ncomp):
            for z in (0, 1, nz + 2, nz + 3):
                lev[c, z, pl.ds(1, tiles), inner] = rim

    def clear(body):
        def step(z, carry):
            for lev in (lev_a, lev_b):
                for c in range(ncomp):
                    body(lev, c, z + 2)
            return carry

        lax.fori_loop(0, nz, step, 0)

    for side in range(2):
        @pl.when(jnp.logical_not(has[side]))
        def _(side=side):
            rows = pl.ds((TOP - 2, TOP + cx)[side], 2)
            def body(lev, c, z):
                lev[c, z, pl.ds(1, tiles), rows] = jnp.zeros((tiles, 2, LANES), jnp.float32)
            clear(body)

        @pl.when(jnp.logical_not(has[2 + side]))
        def _(side=side):
            at = (0, tiles + 1)[side]
            def body(lev, c, z):
                lev[c, z, at, inner] = jnp.zeros((cx, LANES), jnp.float32)
            clear(body)

    def locate():
        count = route_row.shape[1]
        route = route_row[...]
        pick[...] = (
            lax.broadcasted_iota(jnp.int32, (cy, count), 0) == (site_list[...].reshape(1, -1) & (cy - 1))
        ).astype(jnp.float32)
        named = (
            lax.broadcasted_iota(jnp.int32, (n_gx * n_gy, count), 0) == route
        ).astype(jnp.float32)
        earlier = (
            lax.broadcasted_iota(jnp.int32, (count, count), 0)
            < lax.broadcasted_iota(jnp.int32, (count, count), 1)
        ).astype(jnp.float32)
        ahead = jnp.dot(named, earlier, precision=HIGHEST, preferred_element_type=jnp.float32)
        rank = jnp.sum(ahead * named, axis=0, keepdims=True).astype(jnp.int32)
        owner_x = route >> (n_gy.bit_length() - 1)
        owner_y = route & (n_gy - 1)
        spot = owner_y * (n_gx * capacity) + owner_x * capacity + rank
        placing[...] = (
            lax.broadcasted_iota(jnp.int32, (slots, count), 0) == spot
        ).astype(jnp.float32)

    for copy in places_in:
        copy.wait()
    locate()
    pl.semaphore_wait(barrier, n_gx + n_gy - 2)

    def planes(k, t):
        cut = TAIL * (STEPS - k)
        return (0, cut) if t == 0 else (cut, nz)

    def levels(k):
        return (lev_a, lev_b) if k % 2 == 0 else (lev_b, lev_a)

    n_z = n_gx // 2
    column = gx // 2
    even = lax.rem(gx, 2) == 0
    share_left = (4 * column) // n_z
    share_right = (4 * (n_z - 1 - column)) // n_z
    share_sent = jnp.where(even, share_left, share_right)
    share_passed = jnp.where(even, share_right, share_left)

    def pieces(k):
        low, high = planes(k, 1)
        quarter = (high - low + 1) // 4
        return ((low, low + quarter), (low + quarter, low + 2 * quarter), (low + 2 * quarter, high))

    def relayed(piece, share):
        return (lax.rem(share, 2) == 1, False, share >= 2)[piece]

    def strip(k, c, span, row):
        return levels(k)[1].at[c, pl.ds(span[0] + 2, span[1] - span[0]), pl.ds(1, tiles), pl.ds(row, 2)]

    edge_row = (TOP, TOP + cx - 2)
    rim_row = (TOP + cx, TOP - 2)
    step = (-1, 1)

    def halo_copy(k, c, t, d, sending):
        span = planes(k, t)
        if d < 2:
            src = strip(k, c, span, edge_row[d])
            dst = strip(k, c, span, rim_row[d])
            ss, rs = xs_sem, xr_sem
        else:
            lev = levels(k)[1]
            zs = pl.ds(span[0] + 2, span[1] - span[0])
            from_tile, to_tile = ((1, tiles + 1), (tiles, 0))[d - 2]
            src = lev.at[c, zs, from_tile, inner]
            dst = lev.at[c, zs, to_tile, inner]
            ss, rs = ys_sem, yr_sem
        mine = d % 2
        return pltpu.make_async_remote_copy(
            src_ref=src, dst_ref=dst,
            send_sem=ss.at[k, c, t, mine], recv_sem=rs.at[k, c, t, 1 - mine],
            device_id=peer[d if sending else d ^ 1], device_id_type=MESH,
        )

    def piece_copy(k, c, d, piece, by_relay):
        span = pieces(k)[piece]
        rs = pass_sem.at[k, c, piece // 2] if by_relay else xr_sem.at[k, c, 1, 1 - d]
        return pltpu.make_async_remote_copy(
            src_ref=strip(k, c, span, edge_row[d]),
            dst_ref=strip(k, c, span, 2 * (k // 2) if by_relay else rim_row[d]),
            send_sem=xs_sem.at[k, c, 1, d], recv_sem=rs,
            device_id={"gx": gx - step[d] if by_relay else gx + step[d]}, device_id_type=MESH,
        )

    def forward_copy(k, c, piece, d):
        span = pieces(k)[piece]
        return pltpu.make_async_remote_copy(
            src_ref=strip(k, c, span, 2 * (k // 2)), dst_ref=strip(k, c, span, rim_row[d]),
            send_sem=forward_sem.at[k, c, piece // 2], recv_sem=xr_sem.at[k, c, 1, 1 - d],
            device_id={"gx": gx + 2 * step[d]}, device_id_type=MESH,
        )

    def arrival(k, c, piece):
        slot = strip(k, c, pieces(k)[piece], 2 * (k // 2))
        return pltpu.make_async_remote_copy(
            src_ref=slot, dst_ref=slot,
            send_sem=forward_sem.at[k, c, piece // 2], recv_sem=pass_sem.at[k, c, piece // 2],
            device_id={"gx": gx + jnp.where(even, 1, -1)}, device_id_type=MESH,
        )

    def send_halo(k, c, t):
        crosses = (even, jnp.logical_not(even))
        if t == 1:
            for d in range(2):
                for piece in (0, 2):
                    @pl.when(jnp.logical_and(crosses[d], relayed(piece, share_sent)))
                    def _(d=d, piece=piece):
                        piece_copy(k, c, d, piece, True).start()
        for d in range(4):
            if d < 2 and t == 1:
                @pl.when(jnp.logical_and(has[d], crosses[d]))
                def _(d=d):
                    for piece in (0, 2):
                        @pl.when(jnp.logical_not(relayed(piece, share_sent)))
                        def _(piece=piece):
                            piece_copy(k, c, d, piece, False).start()
                    piece_copy(k, c, d, 1, False).start()

                @pl.when(jnp.logical_and(has[d], jnp.logical_not(crosses[d])))
                def _(d=d):
                    halo_copy(k, c, t, d, True).start()
            else:
                @pl.when(has[d])
                def _(d=d):
                    halo_copy(k, c, t, d, True).start()

    def pass_on(k, c):
        for piece in (0, 2):
            @pl.when(relayed(piece, share_passed))
            def _(piece=piece):
                arrival(k, c, piece).wait_recv()
                for d, mine in ((1, even), (0, jnp.logical_not(even))):
                    @pl.when(mine)
                    def _(d=d):
                        forward_copy(k, c, piece, d).start()

    def wait_passed(k, c):
        for piece in (0, 2):
            @pl.when(relayed(piece, share_passed))
            def _(piece=piece):
                arrival(k, c, piece).wait_send()

    def wait_halo(k, c, t):
        for d in range(4):
            @pl.when(has[d ^ 1])
            def _(d=d):
                halo_copy(k, c, t, d, False).wait_recv()

    def wait_sent(k, c, t):
        for d in range(4):
            @pl.when(has[d])
            def _(d=d):
                halo_copy(k, c, t, d, True).wait_send()

    def wave_part(k, c, low, high):
        older, newer = levels(k)

        def group(start, count):
            def put(p, t, half, v, u, old):
                older[c, start + p + 2, t, pl.ds(TOP + half * SUB, SUB)] = v
                if k == STEPS - 1 and low == 0 and p == 0:
                    ground[pl.ds(c * cx + half * SUB, SUB), pl.ds((t - 1) * LANES, LANES)] = (
                        ground_gain * (v - 2.0 * u + old)
                    )

            next_level(newer, older, spd, c, start, count, put)

        each_group(low, high, group)

    def scale_speeds(z, carry):
        own, other = spd[0, z] * (1.0 / 12.0), spd[1, z] * (1.0 / 12.0)
        spd[0, z] = own
        spd[1, z] = other
        spd[2, z] = 2.0 - 30.0 * own - 60.0 * other
        return carry

    def top_step(k, c):
        wait_halo(k, c, 0)
        if k > 0:
            wait_sent(k - 1, c, 0)
        low, high = planes(k, 0)
        wave_part(k, c, low, high)
        if k < STEPS - 1:
            send_halo(k + 1, c, 0)

    def deep_step(k, c):
        pass_on(k, c)
        wait_halo(k, c, 1)
        if k > 0:
            wait_sent(k - 1, c, 1)
        if k == STEPS - 1 and c == ncomp - 1:
            return
        low, high = planes(k, 1)
        wave_part(k, c, low, high)
        if k < STEPS - 1:
            send_halo(k + 1, c, 1)

    wide = 2 * LANES

    def frames(i, carry):
        cols = pl.ds(pl.multiple_of(i * wide, wide), wide)
        frow = lax.broadcasted_iota(jnp.int32, (nf, wide), 0)
        d0, v0, a0 = fd[:, cols], f_vel[:, cols], f_acc[:, cols]
        change = time_step * v0 + 0.5 * time_step * time_step * a0
        nxt = d0 + change
        moving = nxt - d0
        drift = moving - jnp.where(frow < 3, 0.0, pltpu.roll(moving, 3, 0))
        hyst = jnp.clip(fh[:, cols] + drift, -yield_drift, yield_drift)
        fd[:, cols] = nxt
        fh[:, cols] = hyst
        kinds = kind_list[cols].reshape(1, wide)
        total = (-damping) * (v0 + 0.5 * time_step * a0) - hyst_stiff * (
            hyst - jnp.where(frow >= nf - 3, 0.0, pltpu.roll(hyst, nf - 3, 0))
        )
        high, low = split(nxt)
        for kind in range(stiff.shape[0]):
            found = product(stiff_high[kind], high) + (
                product(stiff_high[kind], low) + product(stiff_low[kind], high)
            )
            total = total - jnp.where(kinds == kind, found, 0.0)
        f_acc[:, cols] = total
        f_vel[:, cols] = v0 + 0.5 * time_step * (a0 + total)
        return carry

    def split_stiffness():
        for kind in range(stiff.shape[0]):
            high, low = split(stiff[kind])
            stiff_high[kind] = high
            stiff_low[kind] = low

    def parcel(axis, size, send, recv, ss, rs, off, sending):
        me = place[axis]
        to = lax.rem(me + off, size)
        source = lax.rem(me + size - off, size)
        return pltpu.make_async_remote_copy(
            src_ref=send.at[to],
            dst_ref=recv.at[me if sending else source],
            send_sem=ss.at[off], recv_sem=rs.at[off],
            device_id={axis: to}, device_id_type=MESH,
        )

    hop_1 = ("gy", n_gy, send_1, recv_1, send_1_sem, recv_1_sem)
    hop_2 = ("gx", n_gx, send_2, recv_2, send_2_sem, recv_2_sem)

    def start_hop(hop):
        axis, size, send, recv = hop[:4]
        for off in range(1, size):
            parcel(*hop, off, True).start()
        recv[place[axis]] = send[place[axis]]

    def end_hop(hop):
        for off in range(1, hop[1]):
            parcel(*hop, off, False).wait_recv()

    def post_motion():
        count = route_row.shape[1]
        cells = jnp.dot(
            ground[...], pick[...], precision=HIGHEST, preferred_element_type=jnp.float32
        )
        at_row = lax.broadcasted_iota(jnp.int32, (cx, count), 0) == (
            site_list[...].reshape(1, -1) >> (cy.bit_length() - 1)
        )
        motion = jnp.concatenate(
            [
                jnp.sum(jnp.where(at_row, cells[c * cx:(c + 1) * cx], 0.0), axis=0, keepdims=True)
                for c in range(ncomp)
            ]
            + [jnp.zeros((8 - ncomp, count), jnp.float32)],
            axis=0,
        )
        outgoing = lax.dot_general(
            motion, placing[...], (((1,), (1,)), ((), ())),
            precision=HIGHEST, preferred_element_type=jnp.float32,
        )
        width = n_gx * capacity
        for y in range(n_gy):
            send_1[y] = outgoing[:, y * width:(y + 1) * width]
        start_hop(hop_1)

    part = n_gy * capacity
    narrow = lax.broadcasted_iota(jnp.int32, (8, LANES), 1)

    def relay_motion():
        end_hop(hop_1)
        for x in range(n_gx):
            tile, start = divmod(x * capacity, LANES)
            total = jnp.zeros((8, LANES), jnp.float32)
            for y in range(n_gy):
                piece = recv_1[y, :, tile * LANES:(tile + 1) * LANES]
                shift = (y * capacity - start) % LANES
                if shift:
                    piece = pltpu.roll(piece, shift, 1)
                here = jnp.logical_and(narrow >= y * capacity, narrow < (y + 1) * capacity)
                total = jnp.where(here, piece, total)
            send_2[x] = total
        start_hop(hop_2)

    def add_forcing():
        end_hop(hop_2)
        per_tile = LANES // part
        for tile in range(slots // LANES):
            total = recv_2[tile * per_tile]
            for i in range(1, per_tile):
                piece = pltpu.roll(recv_2[tile * per_tile + i], i * part, 1)
                total = jnp.where(narrow >= i * part, piece, total)
            moved[:, tile * LANES:(tile + 1) * LANES] = total

        def chunk(i, carry):
            cols = pl.ds(pl.multiple_of(i * LANES, LANES), LANES)
            ids = lax.broadcasted_iota(jnp.int32, (nf, LANES), 0)
            phase = ids - 3 * ((ids * 43691) >> 17)
            m = moved[:, cols]
            force = jnp.where(phase == 0, m[0:1], jnp.where(phase == 1, m[1:2], m[2:3]))
            f_acc[:, cols] = f_acc[:, cols] - force
            f_vel[:, cols] = f_vel[:, cols] - (0.5 * time_step) * force
            return carry

        lax.fori_loop(0, slots // LANES, chunk, 0)

    for c in range(ncomp):
        for copy in now_in[c]:
            copy.wait()
        send_halo(0, c, 0)
    send_halo(0, 0, 1)
    for copy in speeds_in:
        copy.wait()
    lax.fori_loop(0, nz, scale_speeds, 0)
    for c in range(ncomp):
        for copy in prev_in[c]:
            copy.wait()
        top_step(0, c)
    send_halo(0, 1, 1)
    for copy in frames_in:
        copy.wait()
    split_stiffness()
    lax.fori_loop(0, slots // wide, frames, 0)
    for c in range(ncomp):
        top_step(1, c)
    send_halo(0, 2, 1)
    deep_step(0, 0)
    for c in range(ncomp):
        top_step(2, c)
    deep_step(0, 1)
    deep_step(0, 2)
    for c in range(ncomp):
        top_step(3, c)
    post_motion()
    deep_step(1, 0)
    relay_motion()
    deep_step(1, 1)
    deep_step(1, 2)
    deep_step(2, 0)
    add_forcing()
    deep_step(2, 1)
    deep_step(2, 2)
    for c in range(ncomp):
        deep_step(3, c)
    for c in range(ncomp):
        for t in range(2):
            wait_sent(STEPS - 1, c, t)
        for k in range(STEPS):
            wait_passed(k, c)
    for hop in (hop_1, hop_2):
        for off in range(1, hop[1]):
            parcel(*hop, off, True).wait_send()


def finish_kernel(
    lev_a, lev_b, spd, fd, f_vel, f_acc, fh, before, last, disp, vel, acc, hyst, fresh, sem,
):
    ncomp, nz, cx, cy = before.shape
    tiles = cy // LANES
    copies = []

    def store(src, dst):
        copy = pltpu.make_async_copy(src, dst, sem.at[len(copies)])
        copy.start()
        copies.append(copy)

    def store_field(lev, out, c, low, high):
        for t in range(tiles):
            store(
                lev.at[c, pl.ds(low + 2, high - low), t + 1, pl.ds(TOP, cx)],
                out.at[c, pl.ds(low, high - low), :, pl.ds(t * LANES, LANES)],
            )

    for c in range(ncomp):
        store_field(lev_a, before, c, 0, nz)
        store_field(lev_b, last, c, 0, nz if c < ncomp - 1 else TAIL)
    for src, dst in ((fd, disp), (f_vel, vel), (f_acc, acc), (fh, hyst)):
        store(src, dst)

    def group(start, count):
        def put(p, t, half, v, u, old):
            fresh[start + p - TAIL, t - 1, pl.ds(half * SUB, SUB)] = v

        next_level(lev_a, lev_b, spd, ncomp - 1, start, count, put)

    cuts = [TAIL, TAIL + 2 * GROUP, nz]
    for low, high in zip(cuts[:-1], cuts[1:]):
        each_group(low, high, group)
        for t in range(tiles):
            store(
                fresh.at[pl.ds(low - TAIL, high - low), t],
                last.at[ncomp - 1, pl.ds(low, high - low), :, pl.ds(t * LANES, LANES)],
            )
    for copy in copies:
        copy.wait()


def shards(
    n_gx, n_gy,
    u_prev, u_now, speeds, sites, routes,
    frame_disp, frame_vel, frame_acc, frame_hyst, frame_kind, stiffness,
):
    ncomp, nz, cx, cy = u_now.shape
    devices = n_gx * n_gy
    nf, slots = frame_disp.shape
    capacity = slots // devices
    count = sites.shape[0]
    tiles = cy // LANES
    f32 = jnp.float32
    i32 = jnp.int32
    bf16 = jnp.bfloat16
    level = pltpu.VMEM((ncomp, nz + 4, tiles + 2, cx + 2 * TOP, LANES), f32)
    batch = pltpu.VMEM((nf, slots), f32)
    first_hop = pltpu.VMEM((n_gy, 8, n_gx * capacity), f32)
    second_hop = pltpu.VMEM((n_gx, 8, LANES), f32)
    halo_sem = pltpu.SemaphoreType.DMA((STEPS, ncomp, 2, 2))
    pass_sem = pltpu.SemaphoreType.DMA((STEPS, ncomp, 2))
    hbm = pl.BlockSpec(memory_space=pltpu.HBM)
    vmem = pl.BlockSpec(memory_space=pltpu.VMEM)
    held = pl.pallas_call(
        functools.partial(wave_kernel, n_gx, n_gy, capacity),
        out_shape=(level, level, pltpu.VMEM((3, nz, tiles, cx, LANES), f32)) + (batch,) * 4,
        in_specs=[hbm] * 11,
        out_specs=(vmem,) * 7,
        scratch_shapes=[
            pltpu.VMEM(stiffness.shape, f32),
            pltpu.VMEM(stiffness.shape, bf16), pltpu.VMEM(stiffness.shape, bf16),
            pltpu.VMEM((count,), i32), pltpu.VMEM((1, count), i32), pltpu.VMEM((slots,), i32),
            pltpu.VMEM((cy, count), f32), pltpu.VMEM((slots, count), f32),
            pltpu.VMEM((ncomp * cx, cy), f32), first_hop, first_hop, second_hop, second_hop,
            pltpu.VMEM((8, slots), f32),
            pltpu.SemaphoreType.DMA((2 * ncomp * tiles + 2 * tiles + 8,)),
            halo_sem, halo_sem, halo_sem, halo_sem, pass_sem, pass_sem,
            pltpu.SemaphoreType.DMA((n_gy,)), pltpu.SemaphoreType.DMA((n_gy,)),
            pltpu.SemaphoreType.DMA((n_gx,)), pltpu.SemaphoreType.DMA((n_gx,)),
        ],
        compiler_params=pltpu.CompilerParams(
            collective_id=0, has_side_effects=True, vmem_limit_bytes=32 * 1024 * 1024
        ),
        name="wave",
    )(
        u_prev, u_now, speeds, sites, routes.reshape(1, count),
        frame_disp, frame_vel, frame_acc, frame_hyst, frame_kind, stiffness,
    )
    field = jax.ShapeDtypeStruct(u_now.shape, f32)
    frame = jax.ShapeDtypeStruct(frame_disp.shape, f32)
    return pl.pallas_call(
        finish_kernel,
        out_shape=(field, field, frame, frame, frame, frame),
        in_specs=[vmem] * 7,
        out_specs=(hbm,) * 6,
        scratch_shapes=[
            pltpu.VMEM((nz - TAIL, tiles, cx, LANES), f32),
            pltpu.SemaphoreType.DMA((2 * ncomp * tiles + 4 + 2 * tiles,)),
        ],
        compiler_params=pltpu.CompilerParams(
            has_side_effects=True, vmem_limit_bytes=4 * 1024 * 1024
        ),
        name="finish",
    )(*held)


def solution(mesh):
    cells = P(None, None, "gx", "gy")
    both = ("gx", "gy")
    frame = P(None, both)
    return jax.shard_map(
        functools.partial(shards, mesh.shape["gx"], mesh.shape["gy"]),
        mesh=mesh,
        in_specs=(cells, cells, cells, P(both), P(both, None), frame, frame, frame, frame,
                  P(both), P()),
        out_specs=(cells, cells, frame, frame, frame, frame),
        check_vma=False,
    )
```

```python
import functools

import jax
import jax.numpy as jnp
from jax import lax
from jax.experimental import pallas as pl
from jax.experimental.pallas import tpu as pltpu
from jax.sharding import PartitionSpec as P

STEPS = 4
time_step = 0.5
damping = 0.1
yield_drift = 0.5
hyst_stiff = 1.0
ground_gain = 0.1
LANES = 128
SUB = 8
TOP = 8
GROUP = 8
TAIL = 2
HIGHEST = lax.Precision.HIGHEST
MESH = pl.DeviceIdType.MESH


def lines(n_gx, n_gy):
    return (("gy", n_gy), ("gx", n_gx))


def split(values):
    high = values.astype(jnp.bfloat16)
    return high, (values - high.astype(jnp.float32)).astype(jnp.bfloat16)


def product(a, b):
    return jnp.dot(a, b, preferred_element_type=jnp.float32)


def each_group(low, high, body):
    whole = (high - low) // GROUP
    rest = low + whole * GROUP

    def group(i, carry):
        body(low + i * GROUP, GROUP)
        return carry

    if whole > 1:
        lax.fori_loop(0, whole, group, 0)
    elif whole:
        body(low, GROUP)
    if rest < high:
        body(rest, high - rest)


def next_level(newer, older, spd, c, start, count, put):
    tiles, cx = newer.shape[2] - 2, newer.shape[3] - 2 * TOP
    lane = lax.broadcasted_iota(jnp.int32, (SUB, LANES), 1)
    for half in range(cx // SUB):
        at = TOP + half * SUB
        rows, local = pl.ds(at, SUB), pl.ds(half * SUB, SUB)
        seen = {}

        def get(t, p):
            if (t, p) not in seen:
                seen[t, p] = newer[c, start + p + 2, t, rows]
            return seen[t, p]

        for t in range(1, tiles + 1):
            for p in range(count):
                u = get(t, p)

                def moved(shift):
                    return newer[c, start + p + 2, t, pl.ds(at + shift, SUB)]

                def turned(i):
                    low = jnp.where(lane >= LANES - i, get(t - 1, p), u)
                    high = jnp.where(lane < i, get(t + 1, p), u)
                    return pltpu.roll(low, i, 1) + pltpu.roll(high, LANES - i, 1)

                ones, twos = [
                    [moved(-i) + moved(i), turned(i), get(t, p - i) + get(t, p + i)]
                    for i in (1, 2)
                ]
                own = 16.0 * ones.pop(c) - twos.pop(c)
                other = 16.0 * (ones[0] + ones[1]) - (twos[0] + twos[1])
                keep, along, across = [spd[i, start + p, t - 1, local] for i in (2, 0, 1)]
                old = older[c, start + p + 2, t, rows]
                v = (keep * u - old) + (along * own + across * other)
                put(p, t, half, v, u, old)


def wave_kernel(
    n_gx, n_gy, capacity,
    u_prev, u_now, speeds, sites, routes,
    frame_disp, frame_vel, frame_acc, frame_hyst, frame_kind, stiffness,
    lev_a, lev_b, spd, fd, f_vel, f_acc, fh,
    stiff, stiff_high, stiff_low, site_list, route_row, kind_list,
    pick, placing, ground, send_1, recv_1, send_2, recv_2, moved,
    load_sem, xs_sem, xr_sem, ys_sem, yr_sem, pass_sem, forward_sem,
    send_1_sem, recv_1_sem, send_2_sem, recv_2_sem,
):
    ncomp, nz, cx, cy = u_now.shape
    tiles = cy // LANES
    nf, slots = fd.shape
    place = {"gx": lax.axis_index("gx"), "gy": lax.axis_index("gy")}
    gx, gy = place["gx"], place["gy"]
    has = (gx > 0, gx < n_gx - 1, gy > 0, gy < n_gy - 1)
    peer = ({"gx": gx - 1}, {"gx": gx + 1}, {"gy": gy - 1}, {"gy": gy + 1})

    loads = []

    def load(src, dst):
        copy = pltpu.make_async_copy(src, dst, load_sem.at[len(loads)])
        copy.start()
        loads.append(copy)
        return copy

    inner = pl.ds(TOP, cx)

    def load_field(src, c, lev):
        return [
            load(
                src.at[c, :, :, pl.ds(t * LANES, LANES)],
                lev.at[c, pl.ds(2, nz), t + 1, inner],
            )
            for t in range(tiles)
        ]

    now_in = [load_field(u_now, c, lev_b) for c in range(ncomp)]
    speeds_in = [
        load(speeds.at[s, :, :, pl.ds(t * LANES, LANES)], spd.at[s, :, t])
        for s in range(2)
        for t in range(tiles)
    ]
    prev_in = [load_field(u_prev, c, lev_a) for c in range(ncomp)]
    frames_in = [
        load(frame_disp, fd), load(frame_vel, f_vel), load(frame_acc, f_acc),
        load(frame_hyst, fh), load(stiffness, stiff), load(frame_kind, kind_list),
    ]
    places_in = [load(sites, site_list), load(routes, route_row)]

    barrier = pltpu.get_barrier_semaphore()
    for axis, size in lines(n_gx, n_gy):
        for off in range(1, size):
            pl.semaphore_signal(
                barrier, inc=1, device_id={axis: lax.rem(place[axis] + off, size)},
                device_id_type=MESH,
            )

    def clear_rims():
        for recv in (recv_1, recv_2):
            spare = recv.shape[1] - ncomp
            recv[:, pl.ds(ncomp, spare)] = jnp.zeros((recv.shape[0], spare, recv.shape[2]), jnp.float32)
        rim = jnp.zeros((tiles, cx, LANES), jnp.float32)
        for lev in (lev_a, lev_b):
            for c in range(ncomp):
                for z in (0, 1, nz + 2, nz + 3):
                    lev[c, z, pl.ds(1, tiles), inner] = rim

        def clear(body):
            def step(z, carry):
                for lev in (lev_a, lev_b):
                    for c in range(ncomp):
                        body(lev, c, z + 2)
                return carry

            lax.fori_loop(0, nz, step, 0)

        for side in range(2):
            @pl.when(jnp.logical_not(has[side]))
            def _(side=side):
                rows = pl.ds((TOP - 2, TOP + cx)[side], 2)
                def body(lev, c, z):
                    lev[c, z, pl.ds(1, tiles), rows] = jnp.zeros((tiles, 2, LANES), jnp.float32)
                clear(body)

            @pl.when(jnp.logical_not(has[2 + side]))
            def _(side=side):
                at = (0, tiles + 1)[side]
                def body(lev, c, z):
                    lev[c, z, at, inner] = jnp.zeros((cx, LANES), jnp.float32)
                clear(body)

    def locate():
        count = route_row.shape[1]
        route = route_row[...]
        pick[...] = (
            lax.broadcasted_iota(jnp.int32, (cy, count), 0) == (site_list[...].reshape(1, -1) & (cy - 1))
        ).astype(jnp.float32)
        named = (
            lax.broadcasted_iota(jnp.int32, (n_gx * n_gy, count), 0) == route
        ).astype(jnp.float32)
        earlier = (
            lax.broadcasted_iota(jnp.int32, (count, count), 0)
            < lax.broadcasted_iota(jnp.int32, (count, count), 1)
        ).astype(jnp.float32)
        ahead = jnp.dot(named, earlier, precision=HIGHEST, preferred_element_type=jnp.float32)
        rank = jnp.sum(ahead * named, axis=0, keepdims=True).astype(jnp.int32)
        owner_x = route >> (n_gy.bit_length() - 1)
        owner_y = route & (n_gy - 1)
        spot = owner_y * (n_gx * capacity) + owner_x * capacity + rank
        placing[...] = (
            lax.broadcasted_iota(jnp.int32, (slots, count), 0) == spot
        ).astype(jnp.float32)

    pl.semaphore_wait(barrier, n_gx + n_gy - 2)

    def planes(k, t):
        cut = TAIL * (STEPS - k)
        return (0, cut) if t == 0 else (cut, nz)

    def levels(k):
        return (lev_a, lev_b) if k % 2 == 0 else (lev_b, lev_a)

    n_z = n_gx // 2
    column = gx // 2
    even = lax.rem(gx, 2) == 0
    share_left = (4 * column) // n_z
    share_right = (4 * (n_z - 1 - column)) // n_z
    share_sent = jnp.where(even, share_left, share_right)
    share_passed = jnp.where(even, share_right, share_left)

    def pieces(k):
        low, high = planes(k, 1)
        quarter = (high - low + 1) // 4
        return (low, low + quarter), (low + 2 * quarter, high)

    def share_at(k, c, share):
        if k < STEPS - 1:
            return share
        return 0 * share if c == ncomp - 1 else share

    def relayed(piece, share):
        return (lax.rem(share, 2) == 1, share >= 2)[piece]

    def direct(k):
        (low, first), (second, high) = pieces(k)
        return ((low, high), (first, high), (low, second), (first, second))

    def strip(k, c, span, row):
        return levels(k)[1].at[c, pl.ds(span[0] + 2, span[1] - span[0]), pl.ds(1, tiles), pl.ds(row, 2)]

    edge_row = (TOP, TOP + cx - 2)
    rim_row = (TOP + cx, TOP - 2)
    step = (-1, 1)

    def halo_copy(k, c, t, d, sending):
        span = planes(k, t)
        if d < 2:
            src = strip(k, c, span, edge_row[d])
            dst = strip(k, c, span, rim_row[d])
            ss, rs = xs_sem, xr_sem
        else:
            lev = levels(k)[1]
            zs = pl.ds(span[0] + 2, span[1] - span[0])
            from_tile, to_tile = ((1, tiles + 1), (tiles, 0))[d - 2]
            src = lev.at[c, zs, from_tile, inner]
            dst = lev.at[c, zs, to_tile, inner]
            ss, rs = ys_sem, yr_sem
        mine = d % 2
        return pltpu.make_async_remote_copy(
            src_ref=src, dst_ref=dst,
            send_sem=ss.at[k, c, t, mine], recv_sem=rs.at[k, c, t, 1 - mine],
            device_id=peer[d if sending else d ^ 1], device_id_type=MESH,
        )

    def piece_copy(k, c, d, piece):
        span = pieces(k)[piece]
        return pltpu.make_async_remote_copy(
            src_ref=strip(k, c, span, edge_row[d]), dst_ref=strip(k, c, span, 2 * (k // 2)),
            send_sem=xs_sem.at[k, c, 1, d], recv_sem=pass_sem.at[k, c, piece],
            device_id={"gx": gx - step[d]}, device_id_type=MESH,
        )

    def direct_copy(k, c, d, span):
        return pltpu.make_async_remote_copy(
            src_ref=strip(k, c, span, edge_row[d]), dst_ref=strip(k, c, span, rim_row[d]),
            send_sem=xs_sem.at[k, c, 1, d], recv_sem=xr_sem.at[k, c, 1, 1 - d],
            device_id={"gx": gx + step[d]}, device_id_type=MESH,
        )

    def forward_copy(k, c, piece, d):
        span = pieces(k)[piece]
        return pltpu.make_async_remote_copy(
            src_ref=strip(k, c, span, 2 * (k // 2)), dst_ref=strip(k, c, span, rim_row[d]),
            send_sem=forward_sem.at[k, c, piece], recv_sem=xr_sem.at[k, c, 1, 1 - d],
            device_id={"gx": gx + 2 * step[d]}, device_id_type=MESH,
        )

    def arrival(k, c, piece):
        slot = strip(k, c, pieces(k)[piece], 2 * (k // 2))
        return pltpu.make_async_remote_copy(
            src_ref=slot, dst_ref=slot,
            send_sem=forward_sem.at[k, c, piece], recv_sem=pass_sem.at[k, c, piece],
            device_id={"gx": gx + jnp.where(even, 1, -1)}, device_id_type=MESH,
        )

    def send_halo(k, c, t):
        crosses = (even, jnp.logical_not(even))
        if t == 1:
            for d in range(2):
                for piece in range(2):
                    @pl.when(jnp.logical_and(crosses[d], relayed(piece, share_at(k, c, share_sent))))
                    def _(d=d, piece=piece):
                        piece_copy(k, c, d, piece).start()
        for d in range(4):
            if d < 2 and t == 1:
                @pl.when(jnp.logical_and(has[d], crosses[d]))
                def _(d=d):
                    for share, span in enumerate(direct(k)):
                        if span[0] < span[1]:
                            @pl.when(share_at(k, c, share_sent) == share)
                            def _(span=span):
                                direct_copy(k, c, d, span).start()

                @pl.when(jnp.logical_and(has[d], jnp.logical_not(crosses[d])))
                def _(d=d):
                    halo_copy(k, c, t, d, True).start()
            else:
                @pl.when(has[d])
                def _(d=d):
                    halo_copy(k, c, t, d, True).start()

    def pass_on(k, c):
        for piece in range(2):
            @pl.when(relayed(piece, share_at(k, c, share_passed)))
            def _(piece=piece):
                arrival(k, c, piece).wait_recv()
                for d, mine in ((1, even), (0, jnp.logical_not(even))):
                    @pl.when(mine)
                    def _(d=d):
                        forward_copy(k, c, piece, d).start()

    def wait_passed(k, c):
        for piece in range(2):
            @pl.when(relayed(piece, share_at(k, c, share_passed)))
            def _(piece=piece):
                arrival(k, c, piece).wait_send()

    def wait_halo(k, c, t):
        for d in range(4):
            @pl.when(has[d ^ 1])
            def _(d=d):
                halo_copy(k, c, t, d, False).wait_recv()

    def wait_sent(k, c, t):
        for d in range(4):
            @pl.when(has[d])
            def _(d=d):
                halo_copy(k, c, t, d, True).wait_send()

    def wave_part(k, c, low, high):
        older, newer = levels(k)

        def group(start, count):
            def put(p, t, half, v, u, old):
                older[c, start + p + 2, t, pl.ds(TOP + half * SUB, SUB)] = v
                if k == STEPS - 1 and low == 0 and p == 0:
                    ground[pl.ds(c * cx + half * SUB, SUB), pl.ds((t - 1) * LANES, LANES)] = (
                        ground_gain * (v - 2.0 * u + old)
                    )

            next_level(newer, older, spd, c, start, count, put)

        each_group(low, high, group)

    def scale_speeds(z, carry):
        own, other = spd[0, z] * (1.0 / 12.0), spd[1, z] * (1.0 / 12.0)
        spd[0, z] = own
        spd[1, z] = other
        spd[2, z] = 2.0 - 30.0 * own - 60.0 * other
        return carry

    def top_step(k, c):
        wait_halo(k, c, 0)
        if k > 0:
            wait_sent(k - 1, c, 0)
        low, high = planes(k, 0)
        wave_part(k, c, low, high)
        if k < STEPS - 1:
            send_halo(k + 1, c, 0)

    def deep_step(k, c):
        if k > 0 or c == ncomp - 1:
            pass_on(k, c)
        wait_halo(k, c, 1)
        if k > 0:
            wait_sent(k - 1, c, 1)
        if k == STEPS - 1 and c == ncomp - 1:
            return
        low, high = planes(k, 1)
        wave_part(k, c, low, high)
        if k < STEPS - 1:
            send_halo(k + 1, c, 1)

    wide = 2 * LANES

    def frames(i, carry):
        cols = pl.ds(pl.multiple_of(i * wide, wide), wide)
        frow = lax.broadcasted_iota(jnp.int32, (nf, wide), 0)
        d0, v0, a0 = fd[:, cols], f_vel[:, cols], f_acc[:, cols]
        change = time_step * v0 + 0.5 * time_step * time_step * a0
        nxt = d0 + change
        moving = nxt - d0
        drift = moving - jnp.where(frow < 3, 0.0, pltpu.roll(moving, 3, 0))
        hyst = jnp.clip(fh[:, cols] + drift, -yield_drift, yield_drift)
        fd[:, cols] = nxt
        fh[:, cols] = hyst
        kinds = kind_list[cols].reshape(1, wide)
        total = (-damping) * (v0 + 0.5 * time_step * a0) - hyst_stiff * (
            hyst - jnp.where(frow >= nf - 3, 0.0, pltpu.roll(hyst, nf - 3, 0))
        )
        high, low = split(nxt)
        for kind in range(stiff.shape[0]):
            found = product(stiff_high[kind], high) + (
                product(stiff_high[kind], low) + product(stiff_low[kind], high)
            )
            total = total - jnp.where(kinds == kind, found, 0.0)
        f_acc[:, cols] = total
        f_vel[:, cols] = v0 + 0.5 * time_step * (a0 + total)
        return carry

    def split_stiffness():
        for kind in range(stiff.shape[0]):
            high, low = split(stiff[kind])
            stiff_high[kind] = high
            stiff_low[kind] = low

    def parcel(axis, size, send, recv, ss, rs, off, sending):
        me = place[axis]
        to = lax.rem(me + off, size)
        source = lax.rem(me + size - off, size)
        return pltpu.make_async_remote_copy(
            src_ref=send.at[to, pl.ds(0, ncomp)],
            dst_ref=recv.at[me if sending else source, pl.ds(0, ncomp)],
            send_sem=ss.at[off], recv_sem=rs.at[off],
            device_id={axis: to}, device_id_type=MESH,
        )

    hop_1 = ("gy", n_gy, send_1, recv_1, send_1_sem, recv_1_sem)
    hop_2 = ("gx", n_gx, send_2, recv_2, send_2_sem, recv_2_sem)

    def start_hop(hop):
        axis, size, send, recv = hop[:4]
        for off in range(1, size):
            parcel(*hop, off, True).start()
        recv[place[axis]] = send[place[axis]]

    def end_hop(hop):
        for off in range(1, hop[1]):
            parcel(*hop, off, False).wait_recv()

    def post_motion():
        count = route_row.shape[1]
        cells = jnp.dot(
            ground[...], pick[...], precision=HIGHEST, preferred_element_type=jnp.float32
        )
        at_row = lax.broadcasted_iota(jnp.int32, (cx, count), 0) == (
            site_list[...].reshape(1, -1) >> (cy.bit_length() - 1)
        )
        motion = jnp.concatenate(
            [
                jnp.sum(jnp.where(at_row, cells[c * cx:(c + 1) * cx], 0.0), axis=0, keepdims=True)
                for c in range(ncomp)
            ]
            + [jnp.zeros((8 - ncomp, count), jnp.float32)],
            axis=0,
        )
        outgoing = lax.dot_general(
            motion, placing[...], (((1,), (1,)), ((), ())),
            precision=HIGHEST, preferred_element_type=jnp.float32,
        )
        width = n_gx * capacity
        for y in range(n_gy):
            send_1[y] = outgoing[:, y * width:(y + 1) * width]
        start_hop(hop_1)

    part = n_gy * capacity
    narrow = lax.broadcasted_iota(jnp.int32, (8, LANES), 1)

    def relay_motion():
        end_hop(hop_1)
        for x in range(n_gx):
            tile, start = divmod(x * capacity, LANES)
            total = jnp.zeros((8, LANES), jnp.float32)
            for y in range(n_gy):
                piece = recv_1[y, :, tile * LANES:(tile + 1) * LANES]
                shift = (y * capacity - start) % LANES
                if shift:
                    piece = pltpu.roll(piece, shift, 1)
                here = jnp.logical_and(narrow >= y * capacity, narrow < (y + 1) * capacity)
                total = jnp.where(here, piece, total)
            send_2[x] = total
        start_hop(hop_2)

    def add_forcing():
        end_hop(hop_2)
        per_tile = LANES // part
        for tile in range(slots // LANES):
            total = recv_2[tile * per_tile]
            for i in range(1, per_tile):
                piece = pltpu.roll(recv_2[tile * per_tile + i], i * part, 1)
                total = jnp.where(narrow >= i * part, piece, total)
            moved[:, tile * LANES:(tile + 1) * LANES] = total

        def chunk(i, carry):
            cols = pl.ds(pl.multiple_of(i * LANES, LANES), LANES)
            ids = lax.broadcasted_iota(jnp.int32, (nf, LANES), 0)
            phase = ids - 3 * ((ids * 43691) >> 17)
            m = moved[:, cols]
            force = jnp.where(phase == 0, m[0:1], jnp.where(phase == 1, m[1:2], m[2:3]))
            f_acc[:, cols] = f_acc[:, cols] - force
            f_vel[:, cols] = f_vel[:, cols] - (0.5 * time_step) * force
            return carry

        lax.fori_loop(0, slots // LANES, chunk, 0)

    for c in range(ncomp):
        for copy in now_in[c]:
            copy.wait()
        send_halo(0, c, 0)
    send_halo(0, 0, 1)
    clear_rims()
    for copy in speeds_in:
        copy.wait()
    lax.fori_loop(0, nz, scale_speeds, 0)
    for c in range(ncomp):
        for copy in prev_in[c]:
            copy.wait()
        top_step(0, c)
    send_halo(0, 1, 1)
    for copy in frames_in:
        copy.wait()
    split_stiffness()
    lax.fori_loop(0, slots // wide, frames, 0)
    for copy in places_in:
        copy.wait()
    locate()
    pass_on(0, 0)
    for c in range(ncomp):
        top_step(1, c)
    send_halo(0, 2, 1)
    deep_step(0, 0)
    pass_on(0, 1)
    for c in range(ncomp):
        top_step(2, c)
    deep_step(0, 1)
    deep_step(0, 2)
    for c in range(ncomp):
        top_step(3, c)
    post_motion()
    deep_step(1, 0)
    relay_motion()
    deep_step(1, 1)
    deep_step(1, 2)
    deep_step(2, 0)
    add_forcing()
    deep_step(2, 1)
    deep_step(2, 2)
    last = ncomp - 1
    for c in range(last):
        deep_step(3, c)
    for hop in (hop_1, hop_2):
        for off in range(1, hop[1]):
            parcel(*hop, off, True).wait_send()
    for c in range(ncomp):
        wait_sent(STEPS - 1, c, 0)
        for k in range(STEPS):
            if k < STEPS - 1 or c < last:
                wait_passed(k, c)
    for c in range(last):
        wait_sent(STEPS - 1, c, 1)
    deep_step(3, last)
    wait_passed(STEPS - 1, last)
    wait_sent(STEPS - 1, last, 1)


def finish_kernel(
    lev_a, lev_b, spd, fd, f_vel, f_acc, fh, before, last, disp, vel, acc, hyst, fresh, sem,
):
    ncomp, nz, cx, cy = before.shape
    tiles = cy // LANES
    copies = []

    def store(src, dst):
        copy = pltpu.make_async_copy(src, dst, sem.at[len(copies)])
        copy.start()
        copies.append(copy)

    def store_field(lev, out, c, low, high):
        for t in range(tiles):
            store(
                lev.at[c, pl.ds(low + 2, high - low), t + 1, pl.ds(TOP, cx)],
                out.at[c, pl.ds(low, high - low), :, pl.ds(t * LANES, LANES)],
            )

    for c in range(ncomp):
        store_field(lev_a, before, c, 0, nz)
        store_field(lev_b, last, c, 0, nz if c < ncomp - 1 else TAIL)
    for src, dst in ((fd, disp), (f_vel, vel), (f_acc, acc), (fh, hyst)):
        store(src, dst)

    def group(start, count):
        def put(p, t, half, v, u, old):
            fresh[start + p - TAIL, t - 1, pl.ds(half * SUB, SUB)] = v

        next_level(lev_a, lev_b, spd, ncomp - 1, start, count, put)

    cuts = [TAIL, TAIL + 2 * GROUP, nz]
    for low, high in zip(cuts[:-1], cuts[1:]):
        each_group(low, high, group)
        for t in range(tiles):
            store(
                fresh.at[pl.ds(low - TAIL, high - low), t],
                last.at[ncomp - 1, pl.ds(low, high - low), :, pl.ds(t * LANES, LANES)],
            )
    for copy in copies:
        copy.wait()


def shards(
    n_gx, n_gy,
    u_prev, u_now, speeds, sites, routes,
    frame_disp, frame_vel, frame_acc, frame_hyst, frame_kind, stiffness,
):
    ncomp, nz, cx, cy = u_now.shape
    devices = n_gx * n_gy
    nf, slots = frame_disp.shape
    capacity = slots // devices
    count = sites.shape[0]
    tiles = cy // LANES
    f32 = jnp.float32
    i32 = jnp.int32
    bf16 = jnp.bfloat16
    level = pltpu.VMEM((ncomp, nz + 4, tiles + 2, cx + 2 * TOP, LANES), f32)
    batch = pltpu.VMEM((nf, slots), f32)
    first_hop = pltpu.VMEM((n_gy, 8, n_gx * capacity), f32)
    second_hop = pltpu.VMEM((n_gx, 8, LANES), f32)
    halo_sem = pltpu.SemaphoreType.DMA((STEPS, ncomp, 2, 2))
    pass_sem = pltpu.SemaphoreType.DMA((STEPS, ncomp, 2))
    hbm = pl.BlockSpec(memory_space=pltpu.HBM)
    vmem = pl.BlockSpec(memory_space=pltpu.VMEM)
    held = pl.pallas_call(
        functools.partial(wave_kernel, n_gx, n_gy, capacity),
        out_shape=(level, level, pltpu.VMEM((3, nz, tiles, cx, LANES), f32)) + (batch,) * 4,
        in_specs=[hbm] * 11,
        out_specs=(vmem,) * 7,
        scratch_shapes=[
            pltpu.VMEM(stiffness.shape, f32),
            pltpu.VMEM(stiffness.shape, bf16), pltpu.VMEM(stiffness.shape, bf16),
            pltpu.VMEM((count,), i32), pltpu.VMEM((1, count), i32), pltpu.VMEM((slots,), i32),
            pltpu.VMEM((cy, count), f32), pltpu.VMEM((slots, count), f32),
            pltpu.VMEM((ncomp * cx, cy), f32), first_hop, first_hop, second_hop, second_hop,
            pltpu.VMEM((8, slots), f32),
            pltpu.SemaphoreType.DMA((2 * ncomp * tiles + 2 * tiles + 8,)),
            halo_sem, halo_sem, halo_sem, halo_sem, pass_sem, pass_sem,
            pltpu.SemaphoreType.DMA((n_gy,)), pltpu.SemaphoreType.DMA((n_gy,)),
            pltpu.SemaphoreType.DMA((n_gx,)), pltpu.SemaphoreType.DMA((n_gx,)),
        ],
        compiler_params=pltpu.CompilerParams(
            collective_id=0, has_side_effects=True, vmem_limit_bytes=32 * 1024 * 1024
        ),
        name="wave",
    )(
        u_prev, u_now, speeds, sites, routes.reshape(1, count),
        frame_disp, frame_vel, frame_acc, frame_hyst, frame_kind, stiffness,
    )
    field = jax.ShapeDtypeStruct(u_now.shape, f32)
    frame = jax.ShapeDtypeStruct(frame_disp.shape, f32)
    return pl.pallas_call(
        finish_kernel,
        out_shape=(field, field, frame, frame, frame, frame),
        in_specs=[vmem] * 7,
        out_specs=(hbm,) * 6,
        scratch_shapes=[
            pltpu.VMEM((nz - TAIL, tiles, cx, LANES), f32),
            pltpu.SemaphoreType.DMA((2 * ncomp * tiles + 4 + 2 * tiles,)),
        ],
        compiler_params=pltpu.CompilerParams(
            has_side_effects=True, vmem_limit_bytes=4 * 1024 * 1024
        ),
        name="finish",
    )(*held)


def solution(mesh):
    cells = P(None, None, "gx", "gy")
    both = ("gx", "gy")
    frame = P(None, both)
    return jax.shard_map(
        functools.partial(shards, mesh.shape["gx"], mesh.shape["gy"]),
        mesh=mesh,
        in_specs=(cells, cells, cells, P(both), P(both, None), frame, frame, frame, frame,
                  P(both), P()),
        out_specs=(cells, cells, frame, frame, frame, frame),
        check_vma=False,
    )
```
